256 devices in a mesh: grp: 8 (over z_lo, core), dev: 32 (over z_hi, x, y).
Axes of the slice: x: 4, y: 4, z: 8 (z_hi: 2, z_lo: 4; z = z_hi * 4 + z_lo), core: 2. Of those that a mesh axis runs over, the one named last changes fastest.
Arguments:
- images: bfloat16 [131072, 64, 128], P(('grp', 'dev')), may hold values from -16 to 16
- test_maps: bfloat16 [64, 128, 32], replicated, may hold values from -6 to 6
- counts: int32 [64], replicated, may hold values from 24 to 64, as said below
Outputs:
- projected: bfloat16 [131072, 64, 32], P(('grp', 'dev'))
The draws below stay inside these ranges and needn't reach their ends.
Inputs may be any that keep to these rules, and one draw needn't show every extreme that they name: `counts`: block 0 has 64 radial functions and block 63 has 24.
All inputs are finite; a program needn't handle non-finite values.
Results may differ from the reference program's by a relative error of at most 0.0049.
Values may be sent and summed in bfloat16 or wider, within the bound.
No kernel may reach another device: no remote copies, remote signals or barrier semaphores. Data moves between devices by JAX's collectives and lax.ppermute only.
A program may use at most 64 MiB of HBM per device.

```python
import jax
import jax.numpy as jnp
from jax import lax

FREQ = 64
R = 64
RANK = 32
RAD_MIN = 24
IMAGES = 131072


def draw_counts(key, part):
    values = jax.random.randint(jax.random.fold_in(key, 7), (FREQ,), RAD_MIN, R + 1)
    values = values.at[0].set(R).at[FREQ - 1].set(RAD_MIN)
    return values.astype(jnp.int32)


def raised(array, key, source, target, parts, factor):
    def block_of(dim):
        return (jnp.arange(array.shape[dim]) // (array.shape[dim] // parts)).reshape((-1,) + (1,) * (array.ndim - 1 - dim))

    one_side = jax.random.permutation(key, parts)[block_of(target)]
    far = (block_of(target) + parts // 2) % parts
    return jnp.where((block_of(source) == one_side) | (block_of(source) == far), factor * array, array)


def block_levels(stream_key, extent, cuts, low, largest):
    def one(dim, blocks):
        heights = jax.random.uniform(jax.random.fold_in(jax.random.fold_in(stream_key, 6), dim), (blocks,), jnp.float32, low / len(cuts), largest / len(cuts))
        return jnp.repeat(jnp.exp(heights), extent[dim] // blocks).reshape((-1,) + (1,) * (len(extent) - dim - 1))

    factor_of = one(*cuts[0])
    for cut in cuts[1:]:
        factor_of = factor_of * one(*cut)
    return factor_of


def noise(rng, extent, scale, bound, split=(), dtype=jnp.bfloat16):
    entries = scale * jax.random.normal(rng, extent, jnp.float32)
    if split:
        entries = entries * block_levels(rng, extent, split, -0.22, 0.18)
    return jnp.clip(entries, -bound, bound).astype(dtype)


def gaussian_with(stream_key, shape, width, most, cuts, heavy, held_as=jnp.bfloat16):
    drawn = width * jax.random.normal(stream_key, shape, jnp.float32)
    if cuts:
        drawn = drawn * block_levels(stream_key, shape, cuts, -0.22, 0.18)
    return jnp.clip(raised(drawn, jax.random.fold_in(stream_key, 3), *heavy), -most, most).astype(held_as)


def setup_inputs(seed: int = 0) -> dict:
    keys = jax.random.split(jax.random.key(seed), 4)
    images = gaussian_with(keys[0], (IMAGES, FREQ, 2 * R), 1.0, 16.0, ((0, 256),), (0, 1, 64, 4.0))
    test_maps = noise(keys[1], (FREQ, 2 * R, RANK), 1.0, 6.0)
    counts = draw_counts(jax.random.fold_in(keys[3], 71), 0)
    return {"images": images, "test_maps": test_maps, "counts": counts}


def orthonormal(summed):
    gram_matrix = jnp.einsum('krs,krt->kst', summed, summed, precision=lax.Precision.HIGHEST)
    factor = jnp.linalg.cholesky(gram_matrix)
    solved = lax.linalg.triangular_solve(factor, summed, left_side=False, lower=True, transpose_a=True)
    return solved.astype(jnp.bfloat16)

def reference(images, test_maps, counts):
    columns = images.shape[2]
    radial = columns // 2
    position = lax.broadcasted_iota(jnp.int32, (images.shape[1], columns), 1) % radial
    valid_mask = (position < counts[:, None]).astype(jnp.bfloat16)
    masked = images * valid_mask[None]
    masked_wide = masked.astype(jnp.float32)
    sketch = jnp.einsum('ikr,krs->iks', masked_wide, test_maps.astype(jnp.float32)).astype(jnp.bfloat16)
    summed = jnp.einsum('ikr,iks->krs', masked_wide, sketch.astype(jnp.float32))
    basis_all = orthonormal(summed)
    projected = jnp.einsum('ikr,krs->iks', masked_wide, basis_all.astype(jnp.float32))
    return projected.astype(jnp.bfloat16)
```

```python
import jax
import jax.numpy as jnp
from jax import lax
from jax.sharding import Mesh, PartitionSpec as P

AXES = ("zl", "co", "zh", "x", "y")
F32, BF16 = jnp.float32, jnp.bfloat16


def orthonormal(summed_t):
    gram_matrix = jnp.einsum("ksr,ktr->kst", summed_t, summed_t, precision=lax.Precision.HIGHEST)
    factor = jnp.linalg.cholesky(gram_matrix)
    solved = lax.linalg.triangular_solve(factor, summed_t, left_side=True, lower=True)
    return solved.astype(BF16)


def body(images, test_maps, counts):
    blocks, columns = images.shape[1], images.shape[2]
    rank = test_maps.shape[2]
    radial = columns // 2
    half, own = blocks // 2, blocks // 32
    core = lax.axis_index("co")
    place = lax.axis_index("x") * 4 + lax.axis_index("y")
    position = lax.broadcasted_iota(jnp.int32, (blocks, columns), 1) % radial
    valid = position < counts[:, None]
    maps_t = jnp.where(valid[:, None, :], jnp.swapaxes(test_maps, 1, 2), 0)
    sketch = jnp.einsum("ikr,ksr->iks", images, maps_t, preferred_element_type=F32).astype(BF16)
    partial = jnp.einsum("iks,ikr->ksr", sketch, images, preferred_element_type=F32)
    swap = [(0, 1), (1, 0)]
    away = lax.dynamic_slice_in_dim(partial, (1 - core) * half, half, 0).astype(BF16)
    kept = lax.dynamic_slice_in_dim(partial, core * half, half, 0)
    pair = (kept + lax.ppermute(away, "co", swap).astype(F32)).astype(BF16)
    parts = lax.all_to_all(pair, ("x", "y"), 0, 0, tiled=True)
    plane = jnp.sum(parts.reshape(16, own, rank, columns).astype(F32), 0).astype(BF16)
    copies = jnp.broadcast_to(plane[None], (8,) + plane.shape)
    parts = lax.all_to_all(copies, ("zl", "zh"), 0, 0, tiled=True)
    total = jnp.sum(parts.astype(F32), 0)
    start = core * half + place * own
    mine = lax.dynamic_slice_in_dim(valid, start, own, 0)
    basis_t = orthonormal(jnp.where(mine[:, None, :], total, 0))
    copies = jnp.broadcast_to(basis_t[None], (16,) + basis_t.shape)
    near = lax.all_to_all(copies, ("x", "y"), 0, 0, tiled=True).reshape(half, rank, columns)
    far = lax.ppermute(near, "co", swap)
    first = core == 0
    bases_t = jnp.concatenate([jnp.where(first, near, far), jnp.where(first, far, near)])
    return jnp.einsum("ikr,ksr->iks", images, bases_t, preferred_element_type=F32).astype(BF16)


def solution(mesh):
    fine = Mesh(mesh.devices.reshape(4, 2, 2, 4, 4), AXES)
    in_specs = (P(AXES, None, None), P(), P())
    out_specs = P(AXES, None, None)
    return jax.shard_map(body, mesh=fine, in_specs=in_specs, out_specs=out_specs, check_vma=False)
```

```python
import functools

import jax
import jax.numpy as jnp
from jax import lax
from jax.experimental import pallas as pl
from jax.experimental.pallas import tpu as pltpu
from jax.sharding import Mesh, PartitionSpec as P

AXES = ("zl", "co", "zh", "x", "y")
F32, BF16 = jnp.float32, jnp.bfloat16
NT = (((1,), (1,)), ((), ()))
STEP = 8


def valid_lanes(count, shape):
    position = lax.broadcasted_iota(jnp.int32, shape, len(shape) - 1) % (shape[-1] // 2)
    return position < count


def diagonal(upper, lower):
    zero = jnp.zeros_like(upper)
    return jnp.concatenate(
        [jnp.concatenate([upper, zero], 1), jnp.concatenate([zero, lower], 1)], 0
    )


def side_by_side(ref, p):
    return jnp.concatenate([ref[2 * p], ref[2 * p + 1]], 1)


def sketch_kernel(info, x_ref, t_ref, away_ref, kept_ref, xo_ref, *, half_steps):
    g = pl.program_id(0)
    blocks, rank, columns = 2 * half_steps * STEP, t_ref.shape[1], t_ref.shape[2]
    group = (g + half_steps * (1 - info[blocks])) % (2 * half_steps)
    xo_ref[...] = pltpu.einshape("ikr->kir", x_ref[...])
    sums = []
    for p in range(STEP // 2):
        pair = side_by_side(xo_ref, p)
        maps = []
        for k in (2 * p, 2 * p + 1):
            valid = valid_lanes(info[group * STEP + k], (rank, columns))
            maps.append(jnp.where(valid, t_ref[k], jnp.zeros((), BF16)))
        sketch = lax.dot_general(diagonal(*maps), pair, NT, preferred_element_type=F32)
        both = jnp.dot(sketch.astype(BF16), pair, preferred_element_type=F32)
        sums += [both[:rank, :columns], both[rank:, columns:]]

    @pl.when(g < half_steps)
    def _():
        for k in range(STEP):
            away_ref[k] = sums[k].astype(BF16)

    @pl.when(g >= half_steps)
    def _():
        for k in range(STEP):
            kept_ref[k] = sums[k]


def sketch_sums(info, images, maps_t):
    count, blocks, columns = images.shape
    rank = maps_t.shape[1]
    steps = blocks // STEP
    half = steps // 2

    def group(g, info):
        return (g + half * (1 - info[blocks])) % steps

    return pl.pallas_call(
        functools.partial(sketch_kernel, half_steps=half),
        out_shape=[
            jax.ShapeDtypeStruct((blocks // 2, rank, columns), BF16),
            jax.ShapeDtypeStruct((blocks // 2, rank, columns), F32),
            jax.ShapeDtypeStruct((blocks, count, columns), BF16),
        ],
        grid_spec=pltpu.PrefetchScalarGridSpec(
            num_scalar_prefetch=1,
            grid=(steps,),
            in_specs=[
                pl.BlockSpec((count, STEP, columns), lambda g, s: (0, group(g, s), 0)),
                pl.BlockSpec((STEP, rank, columns), lambda g, s: (group(g, s), 0, 0)),
            ],
            out_specs=[
                pl.BlockSpec((STEP, rank, columns), lambda g, s: (jnp.minimum(g, half - 1), 0, 0)),
                pl.BlockSpec((STEP, rank, columns), lambda g, s: (jnp.maximum(g - half, 0), 0, 0)),
                pl.BlockSpec((STEP, count, columns), lambda g, s: (group(g, s), 0, 0)),
            ],
        ),
        compiler_params=pltpu.CompilerParams(vmem_limit_bytes=32 << 20),
        cost_estimate=pl.CostEstimate(flops=2**31, bytes_accessed=18 * 2**20, transcendentals=0),
        name="sketch_sums",
    )(info, *[pltpu.with_memory_space_constraint(a, pltpu.HBM) for a in (images, maps_t)])


def combine_kernel(parts_ref, out_ref):
    total = parts_ref[0].astype(F32)
    for i in range(1, parts_ref.shape[0]):
        total = total + parts_ref[i].astype(F32)
    rounded = total.astype(BF16)
    for c in range(out_ref.shape[0]):
        out_ref[c] = rounded


def combine(parts, copies):
    return pl.pallas_call(
        combine_kernel,
        out_shape=jax.ShapeDtypeStruct((copies,) + parts.shape[1:], BF16),
        compiler_params=pltpu.CompilerParams(vmem_limit_bytes=8 << 20),
        name="combine",
    )(parts)


def solve_kernel(info, parts_ref, out_ref):
    copies, own, rank, columns = out_ref.shape
    start = info[info.shape[0] - 1]
    state = []
    for b in range(own):
        total = parts_ref[0, b].astype(F32)
        for i in range(1, parts_ref.shape[0]):
            total = total + parts_ref[i, b].astype(F32)
        total = jnp.where(valid_lanes(info[start + b], (rank, columns)), total, 0.0)
        gram = lax.dot_general(
            total, total, NT, precision=lax.Precision.HIGHEST, preferred_element_type=F32
        )
        state.append((total, gram))
    row = lax.broadcasted_iota(jnp.int32, (rank, 1), 0)
    for j in range(rank):
        for b in range(own):
            total, gram = state[b]
            pivot = gram[j : j + 1, j : j + 1]
            factor = jnp.where(row > j, gram[:, j : j + 1] * (1.0 / pivot), 0.0)
            line = total[j : j + 1, :]
            total = jnp.where(row == j, total * lax.rsqrt(pivot), total - factor * line)
            state[b] = (total, gram - factor * gram[j : j + 1, :])
    for b in range(own):
        rounded = state[b][0].astype(BF16)
        for c in range(copies):
            out_ref[c, b] = rounded


def solve(info, parts, copies):
    return pl.pallas_call(
        solve_kernel,
        out_shape=jax.ShapeDtypeStruct((copies,) + parts.shape[1:], BF16),
        in_specs=[pl.BlockSpec(memory_space=pltpu.SMEM), pl.BlockSpec(memory_space=pltpu.VMEM)],
        out_specs=pl.BlockSpec(memory_space=pltpu.VMEM),
        compiler_params=pltpu.CompilerParams(vmem_limit_bytes=8 << 20),
        name="solve",
    )(info, parts)


def project_kernel(half, x_ref, b_ref, *rest):
    o_ref = rest[-1]
    rank = b_ref.shape[1]
    for p in range(STEP // 2):
        bases = diagonal(b_ref[2 * p], b_ref[2 * p + 1])
        out = lax.dot_general(bases, side_by_side(x_ref, p), NT, preferred_element_type=F32)
        o_ref[2 * p] = out[:rank].astype(BF16)
        o_ref[2 * p + 1] = out[rank:].astype(BF16)


def project(half, rows, bases_t, into=None):
    blocks, count, columns = rows.shape
    rank = bases_t.shape[1]
    steps = blocks // STEP // 2
    extra = [] if into is None else [into]
    return pl.pallas_call(
        project_kernel,
        out_shape=jax.ShapeDtypeStruct((blocks, rank, count), BF16),
        grid_spec=pltpu.PrefetchScalarGridSpec(
            num_scalar_prefetch=1,
            grid=(steps,),
            in_specs=[
                pl.BlockSpec((STEP, count, columns), lambda g, s: (s[0] * steps + g, 0, 0)),
                pl.BlockSpec((STEP, rank, columns), lambda g, s: (g, 0, 0)),
            ]
            + [pl.BlockSpec(memory_space=pl.ANY)] * len(extra),
            out_specs=pl.BlockSpec((STEP, rank, count), lambda g, s: (s[0] * steps + g, 0, 0)),
        ),
        input_output_aliases={3: 0} if extra else {},
        compiler_params=pltpu.CompilerParams(vmem_limit_bytes=16 << 20),
        cost_estimate=pl.CostEstimate(flops=2**28, bytes_accessed=6 * 2**20, transcendentals=0),
        name="project",
    )(half, rows, bases_t, *extra)


def body(images, test_maps, counts):
    blocks, columns = images.shape[1], images.shape[2]
    rank = test_maps.shape[2]
    half, own = blocks // 2, blocks // 32
    core = lax.axis_index("co").astype(jnp.int32)
    place = (lax.axis_index("x") * 4 + lax.axis_index("y")).astype(jnp.int32)
    start = core * half + place * own
    info = jnp.concatenate([counts, core[None], start[None]])
    swap = [(0, 1), (1, 0)]
    away, kept, rows = sketch_sums(info, images, jnp.swapaxes(test_maps, 1, 2))
    pair = (kept + lax.ppermute(away, "co", swap).astype(F32)).astype(BF16)
    parts = lax.all_to_all(pair, ("x", "y"), 0, 0, tiled=True)
    copies = combine(parts.reshape(16, own, rank, columns), 8)
    parts = lax.all_to_all(copies, ("zl", "zh"), 0, 0, tiled=True)
    copies = solve(info, parts, 16)
    near = lax.all_to_all(copies, ("x", "y"), 0, 0, tiled=True).reshape(half, rank, columns)
    far = lax.ppermute(near, "co", swap)
    out = project(core[None], rows, near)
    out = project(1 - core[None], rows, far, out)
    return jnp.transpose(out, (2, 0, 1))


def solution(mesh):
    fine = Mesh(mesh.devices.reshape(4, 2, 2, 4, 4), AXES)
    in_specs = (P(AXES, None, None), P(), P())
    out_specs = P(AXES, None, None)
    return jax.shard_map(body, mesh=fine, in_specs=in_specs, out_specs=out_specs, check_vma=False)
```

```python
import functools

import jax
import jax.numpy as jnp
from jax import lax
from jax.experimental import pallas as pl
from jax.experimental.pallas import tpu as pltpu
from jax.sharding import Mesh, PartitionSpec as P

AXES = ("zl", "co", "zh", "x", "y")
F32, BF16 = jnp.float32, jnp.bfloat16
NT = (((1,), (1,)), ((), ()))
STEP = 8
PANEL = 4


def valid_lanes(count, shape):
    position = lax.broadcasted_iota(jnp.int32, shape, len(shape) - 1) % (shape[-1] // 2)
    return position < count


def diagonal(upper, lower):
    zero = jnp.zeros_like(upper)
    return jnp.concatenate(
        [jnp.concatenate([upper, zero], 1), jnp.concatenate([zero, lower], 1)], 0
    )


def side_by_side(ref, k):
    return jnp.concatenate([ref[k], ref[k + 1]], 1)


def sketch_kernel(counts, images, maps, *refs, half, ahead):
    first = half == "away"
    if first:
        sums_ref, rows_ref, next_ref, count_buf, map_buf, image_buf, sems = refs
    else:
        ready_ref, sums_ref, rows_ref, count_buf, map_buf, image_buf, sems = refs
    halfblocks, rank, columns = sums_ref.shape
    steps = halfblocks // STEP
    core = lax.axis_index("co")
    base = ((1 - core) if first else core) * halfblocks
    other = core * halfblocks

    def images_at(block, target, sem):
        place = pl.multiple_of(block, STEP)
        return pltpu.make_async_copy(images.at[:, pl.ds(place, STEP), :], target, sem)

    copies = []
    if first:
        copies += [images_at(base + g * STEP, image_buf.at[g], sems.at[g]) for g in range(steps)]
        copies += [
            images_at(other + g * STEP, next_ref.at[g], sems.at[steps + g]) for g in range(ahead)
        ]
    else:
        copies += [None] * ahead
        copies += [
            images_at(base + g * STEP, image_buf.at[g - ahead], sems.at[g])
            for g in range(ahead, steps)
        ]
    count_copy = pltpu.make_async_copy(counts, count_buf, sems.at[steps + ahead])
    start = pl.multiple_of(base, STEP)
    map_copy = pltpu.make_async_copy(
        maps.at[pl.ds(start, halfblocks)], map_buf, sems.at[steps + ahead + 1]
    )
    waiting = [copy for copy in copies if copy is not None]
    waiting.pop(0).start()
    count_copy.start()
    map_copy.start()
    waiting.pop(0).start()
    for g in range(steps):
        if copies[g] is None:
            source = ready_ref.at[g]
        else:
            copies[g].wait()
            source = image_buf.at[g if first else g - ahead]
        if waiting:
            waiting.pop(0).start()
        if g == 0:
            count_copy.wait()
            map_copy.wait()
        rows_ref[g * STEP : (g + 1) * STEP] = pltpu.einshape("ikr->kir", source[...])
        for k in range(g * STEP, (g + 1) * STEP, 2):
            pair = side_by_side(rows_ref, k)
            held = []
            for b in (k, k + 1):
                valid = valid_lanes(count_buf[base + b], (rank, columns))
                held.append(jnp.where(valid, map_buf[b], jnp.zeros((), BF16)))
            sketch = lax.dot_general(diagonal(*held), pair, NT, preferred_element_type=F32)
            both = jnp.dot(sketch.astype(BF16), pair, preferred_element_type=F32)
            sums_ref[k] = both[:rank, :columns].astype(sums_ref.dtype)
            sums_ref[k + 1] = both[rank:, columns:].astype(sums_ref.dtype)
    for copy in waiting:
        copy.start()
    if first:
        for copy in copies[steps:]:
            copy.wait()


def sketch_sums(half, counts, images, maps_t, ready=None):
    count, blocks, columns = images.shape
    rank = maps_t.shape[1]
    halfblocks = blocks // 2
    steps = halfblocks // STEP
    ahead = 2
    first = half == "away"
    in_hbm, in_vmem = (pl.BlockSpec(memory_space=m) for m in (pltpu.HBM, pltpu.VMEM))
    out_shape = [
        jax.ShapeDtypeStruct((halfblocks, rank, columns), BF16 if first else F32),
        jax.ShapeDtypeStruct((halfblocks, count, columns), BF16),
    ]
    if first:
        out_shape.append(jax.ShapeDtypeStruct((ahead, count, STEP, columns), BF16))
    extra = [] if first else [ready]
    buffers = steps if first else steps - ahead
    return pl.pallas_call(
        functools.partial(sketch_kernel, half=half, ahead=ahead),
        out_shape=out_shape,
        in_specs=[in_hbm] * 3 + [in_vmem] * len(extra),
        out_specs=[in_vmem] * len(out_shape),
        scratch_shapes=[
            pltpu.SMEM((blocks,), jnp.int32),
            pltpu.VMEM((halfblocks, rank, columns), BF16),
            pltpu.VMEM((buffers, count, STEP, columns), BF16),
            pltpu.SemaphoreType.DMA((steps + ahead + 2,)),
        ],
        compiler_params=pltpu.CompilerParams(vmem_limit_bytes=24 << 20),
        cost_estimate=pl.CostEstimate(flops=2**31, bytes_accessed=6 * 2**20, transcendentals=0),
        name="sketch_" + half,
    )(counts, images, maps_t, *extra)


def combine_kernel(parts_ref, out_ref):
    total = parts_ref[0].astype(F32)
    for i in range(1, parts_ref.shape[0]):
        total = total + parts_ref[i].astype(F32)
    rounded = total.astype(BF16)
    for c in range(out_ref.shape[0]):
        out_ref[c] = rounded


def combine(parts, copies):
    return pl.pallas_call(
        combine_kernel,
        out_shape=jax.ShapeDtypeStruct((copies,) + parts.shape[1:], BF16),
        compiler_params=pltpu.CompilerParams(vmem_limit_bytes=8 << 20),
        name="combine",
    )(parts)


def solve_kernel(counts, parts_ref, out_ref, count_buf, sem):
    copies, own, rank, columns = out_ref.shape
    count_copy = pltpu.make_async_copy(counts, count_buf, sem)
    count_copy.start()
    place = lax.axis_index("x") * 4 + lax.axis_index("y")
    start = lax.axis_index("co") * (counts.shape[0] // 2) + place * own
    totals = []
    for b in range(own):
        total = parts_ref[0, b].astype(F32)
        for i in range(1, parts_ref.shape[0]):
            total = total + parts_ref[i, b].astype(F32)
        totals.append(total)
    count_copy.wait()
    state = []
    for b in range(own):
        total = jnp.where(valid_lanes(count_buf[start + b], (rank, columns)), totals[b], 0.0)
        gram = lax.dot_general(
            total, total, NT, precision=lax.Precision.HIGHEST, preferred_element_type=F32
        )
        state.append((total, gram, jnp.zeros((rank, columns), F32)))
    row = lax.broadcasted_iota(jnp.int32, (rank, columns), 0)
    for panel in range(0, rank, PANEL):
        for b in range(own):
            total, gram, scale = state[b]
            cols = [
                jnp.broadcast_to(gram[:, j : j + 1], (rank, columns))
                for j in range(panel, panel + PANEL)
            ]
            for t in range(PANEL):
                j = panel + t
                pivot = cols[t][j : j + 1, :]
                factor = jnp.where(row > j, cols[t] * (1.0 / pivot), 0.0)
                scale = jnp.where(row == j, lax.rsqrt(pivot), scale)
                total = total - factor * total[j : j + 1, :]
                for u in range(t + 1, PANEL):
                    cols[u] = cols[u] - factor * cols[u][j : j + 1, :]
                gram = gram - factor[:, :rank] * gram[j : j + 1, :]
            state[b] = (total, gram, scale)
    for b in range(own):
        rounded = (state[b][0] * state[b][2]).astype(BF16)
        for c in range(copies):
            out_ref[c, b] = rounded


def solve(counts, parts, copies):
    return pl.pallas_call(
        solve_kernel,
        out_shape=jax.ShapeDtypeStruct((copies,) + parts.shape[1:], BF16),
        in_specs=[pl.BlockSpec(memory_space=pltpu.HBM), pl.BlockSpec(memory_space=pltpu.VMEM)],
        out_specs=pl.BlockSpec(memory_space=pltpu.VMEM),
        scratch_shapes=[pltpu.SMEM(counts.shape, jnp.int32), pltpu.SemaphoreType.DMA],
        compiler_params=pltpu.CompilerParams(vmem_limit_bytes=8 << 20),
        name="solve",
    )(counts, parts)


def project_kernel(rows_ref, bases_ref, *refs, half):
    out_hbm, out_buf, sems = refs[-3:]
    halfblocks, rank, columns = bases_ref.shape
    core = lax.axis_index("co")
    base = (core if half == "near" else 1 - core) * halfblocks
    copies = []
    for g in range(halfblocks // STEP):
        for k in range(g * STEP, (g + 1) * STEP, 2):
            bases = diagonal(bases_ref[k], bases_ref[k + 1])
            pair = side_by_side(rows_ref, k)
            out = lax.dot_general(bases, pair, NT, preferred_element_type=F32).astype(BF16)
            out_buf[k] = out[:rank]
            out_buf[k + 1] = out[rank:]
        done = pl.ds(g * STEP, STEP)
        place = out_hbm.at[pl.ds(base + g * STEP, STEP)]
        copies.append(pltpu.make_async_copy(out_buf.at[done], place, sems.at[g]))
        copies[-1].start()
    for copy in copies:
        copy.wait()


def project(half, rows, bases_t, into=None):
    halfblocks, count, columns = rows.shape
    rank = bases_t.shape[1]
    in_hbm, in_vmem = (pl.BlockSpec(memory_space=m) for m in (pltpu.HBM, pltpu.VMEM))
    extra = [] if into is None else [into]
    return pl.pallas_call(
        functools.partial(project_kernel, half=half),
        out_shape=jax.ShapeDtypeStruct((2 * halfblocks, rank, count), BF16),
        in_specs=[in_vmem] * 2 + [in_hbm] * len(extra),
        out_specs=in_hbm,
        input_output_aliases={2: 0} if extra else {},
        scratch_shapes=[
            pltpu.VMEM((halfblocks, rank, count), BF16),
            pltpu.SemaphoreType.DMA((halfblocks // STEP,)),
        ],
        compiler_params=pltpu.CompilerParams(vmem_limit_bytes=16 << 20),
        cost_estimate=pl.CostEstimate(flops=2**28, bytes_accessed=6 * 2**20, transcendentals=0),
        name="project_" + half,
    )(rows, bases_t, *extra)


def body(images, test_maps, counts):
    blocks, columns = images.shape[1], images.shape[2]
    rank = test_maps.shape[2]
    own = blocks // 32
    swap = [(0, 1), (1, 0)]
    maps_t = jnp.swapaxes(test_maps, 1, 2)
    images, maps_t, counts = [
        pltpu.with_memory_space_constraint(a, pltpu.HBM) for a in (images, maps_t, counts)
    ]
    away, away_rows, ready = sketch_sums("away", counts, images, maps_t)
    other = lax.ppermute(away, "co", swap)
    kept, kept_rows = sketch_sums("kept", counts, images, maps_t, ready)
    pair = (kept + other.astype(F32)).astype(BF16)
    parts = lax.all_to_all(pair, ("x", "y"), 0, 0, tiled=True)
    copies = combine(parts.reshape(16, own, rank, columns), 8)
    parts = lax.all_to_all(copies, ("zl", "zh"), 0, 0, tiled=True)
    copies = solve(counts, parts, 16)
    near = lax.all_to_all(copies, ("x", "y"), 0, 0, tiled=True)
    near = near.reshape(blocks // 2, rank, columns)
    far = lax.ppermute(near, "co", swap)
    out = project("near", kept_rows, near)
    out = project("far", away_rows, far, out)
    return jnp.transpose(out, (2, 0, 1))


def solution(mesh):
    fine = Mesh(mesh.devices.reshape(4, 2, 2, 4, 4), AXES)
    in_specs = (P(AXES, None, None), P(), P())
    out_specs = P(AXES, None, None)
    return jax.shard_map(body, mesh=fine, in_specs=in_specs, out_specs=out_specs, check_vma=False)
```

```python
import functools

import jax
import jax.numpy as jnp
from jax import lax
from jax.experimental import pallas as pl
from jax.experimental.pallas import tpu as pltpu
from jax.sharding import Mesh, PartitionSpec as P

AXES = ("zl", "co", "zh", "x", "y")
F32, BF16 = jnp.float32, jnp.bfloat16
NT = (((1,), (1,)), ((), ()))
STEP = 8
PANEL = 4


def valid_lanes(count, shape):
    position = lax.broadcasted_iota(jnp.int32, shape, len(shape) - 1) % (shape[-1] // 2)
    return position < count


def diagonal(upper, lower):
    zero = jnp.zeros_like(upper)
    return jnp.concatenate(
        [jnp.concatenate([upper, zero], 1), jnp.concatenate([zero, lower], 1)], 0
    )


def side_by_side(ref, k):
    return jnp.concatenate([ref[k], ref[k + 1]], 1)


def sketch_kernel(core, x_ref, t_ref, counts, away_ref, kept_ref, xo_ref, *, half_steps):
    g = pl.program_id(0)
    rank, columns = t_ref.shape[1:]
    group = (g + half_steps * (1 - core[0])) % (2 * half_steps)
    xo_ref[...] = pltpu.einshape("ikr->kir", x_ref[...])
    sums, sketches = [None] * STEP, [None] * (STEP // 2)

    def project_maps(p):
        maps = []
        for k in (2 * p, 2 * p + 1):
            valid = valid_lanes(counts[group * STEP + k], (rank, columns))
            maps.append(jnp.where(valid, t_ref[k], jnp.zeros((), BF16)))
        sketch = lax.dot_general(
            diagonal(*maps), side_by_side(xo_ref, 2 * p), NT, preferred_element_type=F32
        )
        sketches[p] = sketch.astype(BF16)

    def add_up(p):
        pair, sketch = side_by_side(xo_ref, 2 * p), sketches[p]
        both = jnp.dot(sketch, pair, preferred_element_type=F32)
        sums[2 * p] = both[:rank, :columns]
        sums[2 * p + 1] = both[rank:, columns:]

    project_maps(0)
    project_maps(1)
    project_maps(2)
    add_up(0)
    project_maps(3)
    add_up(1)
    add_up(2)
    add_up(3)

    @pl.when(g < half_steps)
    def _():
        for k in range(STEP):
            away_ref[k] = sums[k].astype(BF16)

    @pl.when(g >= half_steps)
    def _():
        for k in range(STEP):
            kept_ref[k] = sums[k]


def sketch_sums(core, counts, images, maps_t):
    count, blocks, columns = images.shape
    rank = maps_t.shape[1]
    steps = blocks // STEP
    half = steps // 2

    def group(g, core):
        return (g + half * (1 - core[0])) % steps

    return pl.pallas_call(
        functools.partial(sketch_kernel, half_steps=half),
        out_shape=[
            jax.ShapeDtypeStruct((blocks // 2, rank, columns), BF16),
            jax.ShapeDtypeStruct((blocks // 2, rank, columns), F32),
            jax.ShapeDtypeStruct((blocks, count, columns), BF16),
        ],
        grid_spec=pltpu.PrefetchScalarGridSpec(
            num_scalar_prefetch=1,
            grid=(steps,),
            in_specs=[
                pl.BlockSpec((count, STEP, columns), lambda g, s: (0, group(g, s), 0)),
                pl.BlockSpec((STEP, rank, columns), lambda g, s: (group(g, s), 0, 0)),
                pl.BlockSpec((blocks,), lambda g, s: (0,), memory_space=pltpu.SMEM),
            ],
            out_specs=[
                pl.BlockSpec((STEP, rank, columns), lambda g, s: (jnp.minimum(g, half - 1), 0, 0)),
                pl.BlockSpec((STEP, rank, columns), lambda g, s: (jnp.maximum(g - half, 0), 0, 0)),
                pl.BlockSpec((STEP, count, columns), lambda g, s: (group(g, s), 0, 0)),
            ],
        ),
        compiler_params=pltpu.CompilerParams(vmem_limit_bytes=32 << 20),
        cost_estimate=pl.CostEstimate(flops=2**31, bytes_accessed=18 * 2**20, transcendentals=0),
        name="sketch_sums",
    )(core, images, maps_t, counts)


def combine_kernel(parts_ref, out_ref):
    total = parts_ref[0].astype(F32)
    for i in range(1, parts_ref.shape[0]):
        total = total + parts_ref[i].astype(F32)
    rounded = total.astype(BF16)
    for c in range(out_ref.shape[0]):
        out_ref[c] = rounded


def combine(parts, copies):
    return pl.pallas_call(
        combine_kernel,
        out_shape=jax.ShapeDtypeStruct((copies,) + parts.shape[1:], BF16),
        compiler_params=pltpu.CompilerParams(vmem_limit_bytes=8 << 20),
        name="combine",
    )(parts)


def solve_kernel(counts, parts_ref, out_ref, count_buf, sem):
    copies, own, rank, columns = out_ref.shape
    count_copy = pltpu.make_async_copy(counts, count_buf, sem)
    count_copy.start()
    place = lax.axis_index("x") * 4 + lax.axis_index("y")
    start = lax.axis_index("co") * (counts.shape[0] // 2) + place * own
    totals = []
    for b in range(own):
        total = parts_ref[0, b].astype(F32)
        for i in range(1, parts_ref.shape[0]):
            total = total + parts_ref[i, b].astype(F32)
        totals.append(total)
    count_copy.wait()
    state = []
    for b in range(own):
        total = jnp.where(valid_lanes(count_buf[start + b], (rank, columns)), totals[b], 0.0)
        gram = lax.dot_general(
            total, total, NT, precision=lax.Precision.HIGHEST, preferred_element_type=F32
        )
        state.append((total, gram, jnp.zeros((rank, columns), F32)))
    row = lax.broadcasted_iota(jnp.int32, (rank, columns), 0)
    for panel in range(0, rank, PANEL):
        for b in range(own):
            total, gram, scale = state[b]
            cols = [
                jnp.broadcast_to(gram[:, j : j + 1], (rank, columns))
                for j in range(panel, panel + PANEL)
            ]
            for t in range(PANEL):
                j = panel + t
                pivot = cols[t][j : j + 1, :]
                factor = jnp.where(row > j, cols[t] * (1.0 / pivot), 0.0)
                scale = jnp.where(row == j, lax.rsqrt(pivot), scale)
                total = total - factor * total[j : j + 1, :]
                for u in range(t + 1, PANEL):
                    cols[u] = cols[u] - factor * cols[u][j : j + 1, :]
                gram = gram - factor[:, :rank] * gram[j : j + 1, :]
            state[b] = (total, gram, scale)
    for b in range(own):
        rounded = (state[b][0] * state[b][2]).astype(BF16)
        for c in range(copies):
            out_ref[c, b] = rounded


def solve(counts, parts, copies):
    return pl.pallas_call(
        solve_kernel,
        out_shape=jax.ShapeDtypeStruct((copies,) + parts.shape[1:], BF16),
        in_specs=[pl.BlockSpec(memory_space=pltpu.HBM), pl.BlockSpec(memory_space=pltpu.VMEM)],
        out_specs=pl.BlockSpec(memory_space=pltpu.VMEM),
        scratch_shapes=[pltpu.SMEM(counts.shape, jnp.int32), pltpu.SemaphoreType.DMA],
        compiler_params=pltpu.CompilerParams(vmem_limit_bytes=8 << 20),
        name="solve",
    )(counts, parts)


def project_kernel(rows_ref, bases_ref, *refs, half):
    out_hbm, out_buf, sems = refs[-3:]
    halfblocks, rank, columns = bases_ref.shape
    core = lax.axis_index("co")
    base = (core if half == "near" else 1 - core) * halfblocks
    copies = []
    for g in range(halfblocks // STEP):
        for k in range(g * STEP, (g + 1) * STEP, 2):
            bases = diagonal(bases_ref[k], bases_ref[k + 1])
            pair = side_by_side(rows_ref, base + k)
            out = lax.dot_general(bases, pair, NT, preferred_element_type=F32).astype(BF16)
            out_buf[k] = out[:rank]
            out_buf[k + 1] = out[rank:]
        done = pl.ds(g * STEP, STEP)
        place = out_hbm.at[pl.ds(base + g * STEP, STEP)]
        copies.append(pltpu.make_async_copy(out_buf.at[done], place, sems.at[g]))
        copies[-1].start()
    for copy in copies:
        copy.wait()


def project(half, rows, bases_t, into=None):
    count = rows.shape[1]
    halfblocks, rank, columns = bases_t.shape
    in_hbm, in_vmem = (pl.BlockSpec(memory_space=m) for m in (pltpu.HBM, pltpu.VMEM))
    extra = [] if into is None else [into]
    return pl.pallas_call(
        functools.partial(project_kernel, half=half),
        out_shape=jax.ShapeDtypeStruct((2 * halfblocks, rank, count), BF16),
        in_specs=[in_vmem] * 2 + [in_hbm] * len(extra),
        out_specs=in_hbm,
        input_output_aliases={2: 0} if extra else {},
        scratch_shapes=[
            pltpu.VMEM((halfblocks, rank, count), BF16),
            pltpu.SemaphoreType.DMA((halfblocks // STEP,)),
        ],
        compiler_params=pltpu.CompilerParams(vmem_limit_bytes=16 << 20),
        cost_estimate=pl.CostEstimate(flops=2**28, bytes_accessed=6 * 2**20, transcendentals=0),
        name="project_" + half,
    )(rows, bases_t, *extra)


def body(images, test_maps, counts):
    blocks, columns = images.shape[1], images.shape[2]
    rank = test_maps.shape[2]
    own = blocks // 32
    swap = [(0, 1), (1, 0)]
    maps_t = jnp.swapaxes(test_maps, 1, 2)
    images, maps_t, counts = [
        pltpu.with_memory_space_constraint(a, pltpu.HBM) for a in (images, maps_t, counts)
    ]
    core = lax.axis_index("co").astype(jnp.int32)[None]
    away, kept, rows = sketch_sums(core, counts, images, maps_t)
    other = lax.ppermute(away, "co", swap)
    pair = (kept + other.astype(F32)).astype(BF16)
    parts = lax.all_to_all(pair, ("x", "y"), 0, 0, tiled=True)
    copies = combine(parts.reshape(16, own, rank, columns), 8)
    parts = lax.all_to_all(copies, ("zl", "zh"), 0, 0, tiled=True)
    copies = solve(counts, parts, 16)
    near = lax.all_to_all(copies, ("x", "y"), 0, 0, tiled=True)
    near = near.reshape(blocks // 2, rank, columns)
    far = lax.ppermute(near, "co", swap)
    out = project("near", rows, near)
    out = project("far", rows, far, out)
    return jnp.transpose(out, (2, 0, 1))


def solution(mesh):
    fine = Mesh(mesh.devices.reshape(4, 2, 2, 4, 4), AXES)
    in_specs = (P(AXES, None, None), P(), P())
    out_specs = P(AXES, None, None)
    return jax.shard_map(body, mesh=fine, in_specs=in_specs, out_specs=out_specs, check_vma=False)
```

```python
import functools

import jax
import jax.numpy as jnp
from jax import lax
from jax.experimental import pallas as pl
from jax.experimental.pallas import tpu as pltpu
from jax.sharding import Mesh, PartitionSpec as P

AXES = ("zl", "co", "zh", "x", "y")
F32, BF16 = jnp.float32, jnp.bfloat16
NT = (((1,), (1,)), ((), ()))
TILE = 8
STEP = 16
WRITE = 4
PANEL = 4


def valid_lanes(count, shape):
    position = lax.broadcasted_iota(jnp.int32, shape, len(shape) - 1) % (shape[-1] // 2)
    return position < count


def diagonal(upper, lower):
    zero = jnp.zeros_like(upper)
    return jnp.concatenate(
        [jnp.concatenate([upper, zero], 1), jnp.concatenate([zero, lower], 1)], 0
    )


def side_by_side(ref, k):
    return jnp.concatenate([ref[k], ref[k + 1]], 1)


def sketch_kernel(core, xa_ref, xb_ref, t_ref, counts, away_ref, kept_ref, xo_ref, *, half_steps):
    g = pl.program_id(0)
    rank, columns = t_ref.shape[1:]
    group = (g + half_steps * (1 - core[0])) % (2 * half_steps)
    sums, sketches = [None] * STEP, [None] * (STEP // 2)
    valid = [valid_lanes(counts[group * STEP + k], (rank, columns)) for k in range(STEP)]

    def project_maps(p):
        maps = []
        for k in (2 * p, 2 * p + 1):
            maps.append(jnp.where(valid[k], t_ref[k], jnp.zeros((), BF16)))
        sketch = lax.dot_general(
            diagonal(*maps), side_by_side(xo_ref, 2 * p), NT, preferred_element_type=F32
        )
        sketches[p] = sketch.astype(BF16)

    def add_up(p):
        pair, sketch = side_by_side(xo_ref, 2 * p), sketches[p]
        both = jnp.dot(sketch, pair, preferred_element_type=F32)
        sums[2 * p] = jnp.where(valid[2 * p], both[:rank, :columns], 0.0)
        sums[2 * p + 1] = jnp.where(valid[2 * p + 1], both[rank:, columns:], 0.0)

    xo_ref[:TILE] = pltpu.einshape("ikr->kir", xa_ref[...])
    xo_ref[TILE:] = pltpu.einshape("ikr->kir", xb_ref[...])
    project_maps(0)
    project_maps(1)
    project_maps(2)
    project_maps(3)
    project_maps(4)
    project_maps(5)
    project_maps(6)
    project_maps(7)
    add_up(0)
    add_up(1)
    add_up(2)
    add_up(3)
    add_up(4)
    add_up(5)
    add_up(6)
    add_up(7)

    @pl.when(g < half_steps)
    def _():
        for k in range(STEP):
            away_ref[k] = sums[k].astype(BF16)

    @pl.when(g >= half_steps)
    def _():
        for k in range(STEP):
            kept_ref[k] = sums[k]


def sketch_sums(core, counts, images, maps_t):
    count, blocks, columns = images.shape
    rank = maps_t.shape[1]
    steps = blocks // STEP
    half = steps // 2

    def group(g, core):
        return (g + half * (1 - core[0])) % steps

    return pl.pallas_call(
        functools.partial(sketch_kernel, half_steps=half),
        out_shape=[
            jax.ShapeDtypeStruct((blocks // 2, rank, columns), BF16),
            jax.ShapeDtypeStruct((blocks // 2, rank, columns), F32),
            jax.ShapeDtypeStruct((blocks, count, columns), BF16),
        ],
        grid_spec=pltpu.PrefetchScalarGridSpec(
            num_scalar_prefetch=1,
            grid=(steps,),
            in_specs=[
                pl.BlockSpec((count, TILE, columns), lambda g, s: (0, 2 * group(g, s), 0)),
                pl.BlockSpec((count, TILE, columns), lambda g, s: (0, 2 * group(g, s) + 1, 0)),
                pl.BlockSpec((STEP, rank, columns), lambda g, s: (group(g, s), 0, 0)),
                pl.BlockSpec((blocks,), lambda g, s: (0,), memory_space=pltpu.SMEM),
            ],
            out_specs=[
                pl.BlockSpec((STEP, rank, columns), lambda g, s: (jnp.minimum(g, half - 1), 0, 0)),
                pl.BlockSpec((STEP, rank, columns), lambda g, s: (jnp.maximum(g - half, 0), 0, 0)),
                pl.BlockSpec((STEP, count, columns), lambda g, s: (group(g, s), 0, 0)),
            ],
        ),
        compiler_params=pltpu.CompilerParams(vmem_limit_bytes=32 << 20),
        cost_estimate=pl.CostEstimate(flops=2**31, bytes_accessed=18 * 2**20, transcendentals=0),
        name="sketch_sums",
    )(core, images, images, maps_t, counts)


def combine_kernel(parts_ref, out_ref):
    total = parts_ref[0].astype(F32)
    for i in range(1, parts_ref.shape[0]):
        total = total + parts_ref[i].astype(F32)
    rounded = total.astype(BF16)
    for c in range(out_ref.shape[0]):
        out_ref[c] = rounded


def combine(parts, copies):
    return pl.pallas_call(
        combine_kernel,
        out_shape=jax.ShapeDtypeStruct((copies,) + parts.shape[1:], BF16),
        compiler_params=pltpu.CompilerParams(vmem_limit_bytes=8 << 20),
        name="combine",
    )(parts)


def solve_kernel(parts_ref, out_ref):
    copies, own, rank, columns = out_ref.shape
    state = []
    for b in range(own):
        total = parts_ref[0, b].astype(F32)
        for i in range(1, parts_ref.shape[0]):
            total = total + parts_ref[i, b].astype(F32)
        gram = lax.dot_general(
            total, total, NT, precision=lax.Precision.HIGHEST, preferred_element_type=F32
        )
        state.append((total, gram, jnp.zeros((rank, columns), F32)))
    row = lax.broadcasted_iota(jnp.int32, (rank, columns), 0)
    for panel in range(0, rank, PANEL):
        for b in range(own):
            total, gram, scale = state[b]
            cols = [
                jnp.broadcast_to(gram[:, j : j + 1], (rank, columns))
                for j in range(panel, panel + PANEL)
            ]
            for t in range(PANEL):
                j = panel + t
                pivot = cols[t][j : j + 1, :]
                factor = jnp.where(row > j, cols[t] * (1.0 / pivot), 0.0)
                scale = jnp.where(row == j, lax.rsqrt(pivot), scale)
                total = total - factor * total[j : j + 1, :]
                for u in range(t + 1, PANEL):
                    cols[u] = cols[u] - factor * cols[u][j : j + 1, :]
                gram = gram - factor[:, :rank] * gram[j : j + 1, :]
            state[b] = (total, gram, scale)
    for b in range(own):
        rounded = (state[b][0] * state[b][2]).astype(BF16)
        for c in range(copies):
            out_ref[c, b] = rounded


def solve(parts, copies):
    return pl.pallas_call(
        solve_kernel,
        out_shape=jax.ShapeDtypeStruct((copies,) + parts.shape[1:], BF16),
        compiler_params=pltpu.CompilerParams(
            vmem_limit_bytes=8 << 20
        ),
        name="solve",
    )(parts)


def project_pair(rows_ref, base, bases_ref, k, out_ref):
    rank = bases_ref.shape[1]
    bases = diagonal(bases_ref[k], bases_ref[k + 1])
    pair = side_by_side(rows_ref, base + k)
    out = lax.dot_general(bases, pair, NT, preferred_element_type=F32).astype(BF16)
    out_ref[k] = out[:rank]
    out_ref[k + 1] = out[rank:]


def near_kernel(rows_ref, bases_ref, out_ref):
    blocks = bases_ref.shape[0]
    base = lax.axis_index("co") * blocks
    for k in range(0, blocks, 2):
        project_pair(rows_ref, base, bases_ref, k, out_ref)


def far_kernel(rows_ref, bases_ref, near_ref, out_hbm, out_buf, sems):
    blocks = bases_ref.shape[0]
    core = lax.axis_index("co")
    base = (1 - core) * blocks
    place = out_hbm.at[pl.ds(core * blocks, blocks)]
    copies = [pltpu.make_async_copy(near_ref, place, sems.at[0])]
    copies[0].start()
    for first in range(0, blocks, WRITE):
        for k in range(first, first + WRITE, 2):
            project_pair(rows_ref, base, bases_ref, k, out_buf)
        place = out_hbm.at[pl.ds(base + first, WRITE)]
        sem = sems.at[1 + first // WRITE]
        copies.append(pltpu.make_async_copy(out_buf.at[pl.ds(first, WRITE)], place, sem))
        copies[-1].start()
    for copy in copies:
        copy.wait()


def project(rows, near, far):
    count = rows.shape[1]
    half, rank, columns = near.shape
    in_hbm, in_vmem = (pl.BlockSpec(memory_space=m) for m in (pltpu.HBM, pltpu.VMEM))
    settings = dict(
        compiler_params=pltpu.CompilerParams(vmem_limit_bytes=16 << 20),
        cost_estimate=pl.CostEstimate(flops=2**28, bytes_accessed=6 * 2**20, transcendentals=0),
    )
    done = pl.pallas_call(
        near_kernel,
        out_shape=jax.ShapeDtypeStruct((half, rank, count), BF16),
        in_specs=[in_vmem] * 2,
        out_specs=in_vmem,
        name="project_near",
        **settings,
    )(rows, near)
    return pl.pallas_call(
        far_kernel,
        out_shape=jax.ShapeDtypeStruct((2 * half, rank, count), BF16),
        in_specs=[in_vmem] * 3,
        out_specs=in_hbm,
        scratch_shapes=[
            pltpu.VMEM((half, rank, count), BF16),
            pltpu.SemaphoreType.DMA((1 + half // WRITE,)),
        ],
        name="project_far",
        **settings,
    )(rows, far, done)


def body(images, test_maps, counts):
    blocks, columns = images.shape[1], images.shape[2]
    rank = test_maps.shape[2]
    own = blocks // 32
    swap = [(0, 1), (1, 0)]
    maps_t = jnp.swapaxes(test_maps, 1, 2)
    images, maps_t, counts = [
        pltpu.with_memory_space_constraint(a, pltpu.HBM) for a in (images, maps_t, counts)
    ]
    core = lax.axis_index("co").astype(jnp.int32)[None]
    away, kept, rows = sketch_sums(core, counts, images, maps_t)
    other = lax.ppermute(away, "co", swap)
    pair = (kept + other.astype(F32)).astype(BF16)
    parts = lax.all_to_all(pair, ("x", "y"), 0, 0, tiled=True)
    copies = combine(parts.reshape(16, own, rank, columns), 8)
    parts = lax.all_to_all(copies, ("zl", "zh"), 0, 0, tiled=True)
    copies = solve(parts, 16)
    near = lax.all_to_all(copies, ("x", "y"), 0, 0, tiled=True)
    near = near.reshape(blocks // 2, rank, columns)
    out = project(rows, near, lax.ppermute(near, "co", swap))
    return jnp.transpose(out, (2, 0, 1))


def solution(mesh):
    fine = Mesh(mesh.devices.reshape(4, 2, 2, 4, 4), AXES)
    in_specs = (P(AXES, None, None), P(), P())
    out_specs = P(AXES, None, None)
    return jax.shard_map(body, mesh=fine, in_specs=in_specs, out_specs=out_specs, check_vma=False)
```

```python
import functools

import jax
import jax.numpy as jnp
from jax import lax
from jax.experimental import pallas as pl
from jax.experimental.pallas import tpu as pltpu
from jax.sharding import Mesh, PartitionSpec as P

AXES = ("zl", "co", "zh", "x", "y")
F32, BF16 = jnp.float32, jnp.bfloat16
NT = (((1,), (1,)), ((), ()))
TILE = 8
STEP = 16
WRITE = 4
PANEL = 4


def valid_lanes(count, shape):
    position = lax.broadcasted_iota(jnp.int32, shape, len(shape) - 1) % (shape[-1] // 2)
    return position < count


def diagonal(upper, lower):
    zero = jnp.zeros_like(upper)
    return jnp.concatenate(
        [jnp.concatenate([upper, zero], 1), jnp.concatenate([zero, lower], 1)], 0
    )


def side_by_side(ref, k):
    return jnp.concatenate([ref[k], ref[k + 1]], 1)


def sketch_kernel(core, xa_ref, xb_ref, t_ref, counts, away_ref, kept_ref, xo_ref, *, half_steps):
    g = pl.program_id(0)
    rank, columns = t_ref.shape[1:]
    group = (g + half_steps * (1 - core[0])) % (2 * half_steps)
    sums, sketches = [None] * STEP, [None] * (STEP // 2)
    valid = [valid_lanes(counts[group * STEP + k], (rank, columns)) for k in range(STEP)]

    def project_maps(p):
        maps = []
        for k in (2 * p, 2 * p + 1):
            maps.append(jnp.where(valid[k], t_ref[k], jnp.zeros((), BF16)))
        sketch = lax.dot_general(
            diagonal(*maps), side_by_side(xo_ref, 2 * p), NT, preferred_element_type=F32
        )
        sketches[p] = sketch.astype(BF16)

    def add_up(p):
        pair, sketch = side_by_side(xo_ref, 2 * p), sketches[p]
        both = jnp.dot(sketch, pair, preferred_element_type=F32)
        sums[2 * p] = jnp.where(valid[2 * p], both[:rank, :columns], 0.0)
        sums[2 * p + 1] = jnp.where(valid[2 * p + 1], both[rank:, columns:], 0.0)

    xo_ref[TILE:] = pltpu.einshape("ikr->kir", xb_ref[...])
    xo_ref[:TILE] = pltpu.einshape("ikr->kir", xa_ref[...])
    project_maps(0)
    project_maps(1)
    project_maps(2)
    project_maps(3)
    project_maps(4)
    project_maps(5)
    add_up(0)
    add_up(1)
    project_maps(6)
    project_maps(7)
    add_up(2)
    add_up(3)
    add_up(4)
    add_up(5)
    add_up(6)
    add_up(7)

    @pl.when(g < half_steps)
    def _():
        for k in range(STEP):
            away_ref[k] = sums[k].astype(BF16)

    @pl.when(g >= half_steps)
    def _():
        for k in range(STEP):
            kept_ref[k] = sums[k]


def sketch_sums(core, counts, images, maps_t):
    count, blocks, columns = images.shape
    rank = maps_t.shape[1]
    steps = blocks // STEP
    half = steps // 2

    def group(g, core):
        return (g + half * (1 - core[0])) % steps

    return pl.pallas_call(
        functools.partial(sketch_kernel, half_steps=half),
        out_shape=[
            jax.ShapeDtypeStruct((blocks // 2, rank, columns), BF16),
            jax.ShapeDtypeStruct((blocks // 2, rank, columns), F32),
            jax.ShapeDtypeStruct((blocks, count, columns), BF16),
        ],
        grid_spec=pltpu.PrefetchScalarGridSpec(
            num_scalar_prefetch=1,
            grid=(steps,),
            in_specs=[
                pl.BlockSpec((count, TILE, columns), lambda g, s: (0, 2 * group(g, s), 0)),
                pl.BlockSpec((count, TILE, columns), lambda g, s: (0, 2 * group(g, s) + 1, 0)),
                pl.BlockSpec((STEP, rank, columns), lambda g, s: (group(g, s), 0, 0)),
                pl.BlockSpec((blocks,), lambda g, s: (0,), memory_space=pltpu.SMEM),
            ],
            out_specs=[
                pl.BlockSpec((STEP, rank, columns), lambda g, s: (jnp.minimum(g, half - 1), 0, 0)),
                pl.BlockSpec((STEP, rank, columns), lambda g, s: (jnp.maximum(g - half, 0), 0, 0)),
                pl.BlockSpec((STEP, count, columns), lambda g, s: (group(g, s), 0, 0)),
            ],
        ),
        compiler_params=pltpu.CompilerParams(vmem_limit_bytes=32 << 20),
        cost_estimate=pl.CostEstimate(flops=2**31, bytes_accessed=18 * 2**20, transcendentals=0),
        name="sketch_sums",
    )(core, images, images, maps_t, counts)


def combine_kernel(parts_ref, out_ref):
    total = parts_ref[0].astype(F32)
    for i in range(1, parts_ref.shape[0]):
        total = total + parts_ref[i].astype(F32)
    rounded = total.astype(BF16)
    for c in range(out_ref.shape[0]):
        out_ref[c] = rounded


def combine(parts, copies):
    return pl.pallas_call(
        combine_kernel,
        out_shape=jax.ShapeDtypeStruct((copies,) + parts.shape[1:], BF16),
        compiler_params=pltpu.CompilerParams(vmem_limit_bytes=8 << 20),
        name="combine",
    )(parts)


def solve_kernel(parts_ref, out_ref):
    copies, own, rank, columns = out_ref.shape
    state = []
    for b in range(own):
        total = parts_ref[0, b].astype(F32)
        for i in range(1, parts_ref.shape[0]):
            total = total + parts_ref[i, b].astype(F32)
        gram = lax.dot_general(
            total, total, NT, precision=lax.Precision.HIGHEST, preferred_element_type=F32
        )
        state.append((total, gram, jnp.zeros((rank, columns), F32)))
    row = lax.broadcasted_iota(jnp.int32, (rank, columns), 0)
    for panel in range(0, rank, PANEL):
        for b in range(own):
            total, gram, scale = state[b]
            cols = [
                jnp.broadcast_to(gram[:, j : j + 1], (rank, columns))
                for j in range(panel, panel + PANEL)
            ]
            for t in range(PANEL):
                j = panel + t
                pivot = cols[t][j : j + 1, :]
                factor = jnp.where(row > j, cols[t] * (1.0 / pivot), 0.0)
                scale = jnp.where(row == j, lax.rsqrt(pivot), scale)
                total = total - factor * total[j : j + 1, :]
                for u in range(t + 1, PANEL):
                    cols[u] = cols[u] - factor * cols[u][j : j + 1, :]
                gram = gram - factor[:, :rank] * gram[j : j + 1, :]
            state[b] = (total, gram, scale)
    for b in range(own):
        rounded = (state[b][0] * state[b][2]).astype(BF16)
        for c in range(copies):
            out_ref[c, b] = rounded


def solve(parts, copies):
    return pl.pallas_call(
        solve_kernel,
        out_shape=jax.ShapeDtypeStruct((copies,) + parts.shape[1:], BF16),
        compiler_params=pltpu.CompilerParams(
            vmem_limit_bytes=8 << 20
        ),
        name="solve",
    )(parts)


def project_pair(rows_ref, base, bases_ref, k, out_ref):
    rank = bases_ref.shape[1]
    bases = diagonal(bases_ref[k], bases_ref[k + 1])
    pair = side_by_side(rows_ref, base + k)
    out = lax.dot_general(bases, pair, NT, preferred_element_type=F32).astype(BF16)
    out_ref[k] = out[:rank]
    out_ref[k + 1] = out[rank:]


def near_kernel(rows_ref, bases_ref, out_ref):
    blocks = bases_ref.shape[0]
    base = lax.axis_index("co") * blocks
    for k in range(0, blocks, 2):
        project_pair(rows_ref, base, bases_ref, k, out_ref)


def far_kernel(rows_ref, bases_ref, near_ref, out_hbm, out_buf, sems):
    blocks = bases_ref.shape[0]
    core = lax.axis_index("co")
    base = (1 - core) * blocks
    place = out_hbm.at[pl.ds(core * blocks, blocks)]
    copies = [pltpu.make_async_copy(near_ref, place, sems.at[0])]
    copies[0].start()
    for first in range(0, blocks, WRITE):
        for k in range(first, first + WRITE, 2):
            project_pair(rows_ref, base, bases_ref, k, out_buf)
        place = out_hbm.at[pl.ds(base + first, WRITE)]
        sem = sems.at[1 + first // WRITE]
        copies.append(pltpu.make_async_copy(out_buf.at[pl.ds(first, WRITE)], place, sem))
        copies[-1].start()
    for copy in copies:
        copy.wait()


def project(rows, near, far):
    count = rows.shape[1]
    half, rank, columns = near.shape
    in_hbm, in_vmem = (pl.BlockSpec(memory_space=m) for m in (pltpu.HBM, pltpu.VMEM))
    settings = dict(
        compiler_params=pltpu.CompilerParams(vmem_limit_bytes=16 << 20),
        cost_estimate=pl.CostEstimate(flops=2**28, bytes_accessed=6 * 2**20, transcendentals=0),
    )
    done = pl.pallas_call(
        near_kernel,
        out_shape=jax.ShapeDtypeStruct((half, rank, count), BF16),
        in_specs=[in_vmem] * 2,
        out_specs=in_vmem,
        name="project_near",
        **settings,
    )(rows, near)
    return pl.pallas_call(
        far_kernel,
        out_shape=jax.ShapeDtypeStruct((2 * half, rank, count), BF16),
        in_specs=[in_vmem] * 3,
        out_specs=in_hbm,
        scratch_shapes=[
            pltpu.VMEM((half, rank, count), BF16),
            pltpu.SemaphoreType.DMA((1 + half // WRITE,)),
        ],
        name="project_far",
        **settings,
    )(rows, far, done)


def body(images, test_maps, counts):
    blocks, columns = images.shape[1], images.shape[2]
    rank = test_maps.shape[2]
    own = blocks // 32
    swap = [(0, 1), (1, 0)]
    maps_t = jnp.swapaxes(test_maps, 1, 2)
    images, maps_t, counts = [
        pltpu.with_memory_space_constraint(a, pltpu.HBM) for a in (images, maps_t, counts)
    ]
    core = lax.axis_index("co").astype(jnp.int32)[None]
    away, kept, rows = sketch_sums(core, counts, images, maps_t)
    other = lax.ppermute(away, "co", swap)
    pair = (kept + other.astype(F32)).astype(BF16)
    parts = lax.all_to_all(pair, ("y", "x"), 0, 0, tiled=True)
    copies = combine(parts.reshape(16, own, rank, columns), 8)
    parts = lax.all_to_all(copies, ("zl", "zh"), 0, 0, tiled=True)
    copies = solve(parts, 16)
    near = lax.all_to_all(copies, ("y", "x"), 0, 0, tiled=True)
    near = near.reshape(blocks // 2, rank, columns)
    out = project(rows, near, lax.ppermute(near, "co", swap))
    return jnp.transpose(out, (2, 0, 1))


def solution(mesh):
    fine = Mesh(mesh.devices.reshape(4, 2, 2, 4, 4), AXES)
    in_specs = (P(AXES, None, None), P(), P())
    out_specs = P(AXES, None, None)
    return jax.shard_map(body, mesh=fine, in_specs=in_specs, out_specs=out_specs, check_vma=False)
```

```python
import functools

import jax
import jax.numpy as jnp
from jax import lax
from jax.experimental import pallas as pl
from jax.experimental.pallas import tpu as pltpu
from jax.sharding import Mesh, PartitionSpec as P

AXES = ("zl", "co", "zh", "x", "y")
F32, BF16 = jnp.float32, jnp.bfloat16
NT = (((1,), (1,)), ((), ()))
TILE = 8
STEP = 16
WRITE = 4
PANEL = 4


def valid_lanes(count, shape):
    position = lax.broadcasted_iota(jnp.int32, shape, len(shape) - 1) % (shape[-1] // 2)
    return position < count


def diagonal(upper, lower):
    zero = jnp.zeros_like(upper)
    return jnp.concatenate(
        [jnp.concatenate([upper, zero], 1), jnp.concatenate([zero, lower], 1)], 0
    )


def side_by_side(ref, k):
    return jnp.concatenate([ref[k], ref[k + 1]], 1)


def sketch_step(tiles, maps_ref, valid, rows_ref, sums_ref, base):
    rank, columns = maps_ref.shape[1:]
    sketches = [None] * (STEP // 2)

    def project_maps(p):
        maps = [
            jnp.where(valid[k], maps_ref[base + k], jnp.zeros((), BF16)) for k in (2 * p, 2 * p + 1)
        ]
        pair = side_by_side(rows_ref, base + 2 * p)
        sketch = lax.dot_general(diagonal(*maps), pair, NT, preferred_element_type=F32)
        sketches[p] = sketch.astype(BF16)

    def add_up(p):
        pair = side_by_side(rows_ref, base + 2 * p)
        both = jnp.dot(sketches[p], pair, preferred_element_type=F32)
        for h in range(2):
            own = both[h * rank : (h + 1) * rank, h * columns : (h + 1) * columns]
            own = jnp.where(valid[2 * p + h], own, 0.0)
            sums_ref[base + 2 * p + h] = own.astype(sums_ref.dtype)

    for h in (1, 0):
        rows_ref[base + h * TILE : base + (h + 1) * TILE] = pltpu.einshape("ikr->kir", tiles[h][...])
    for p in range(6):
        project_maps(p)
    for p in range(2):
        add_up(p)
    for p in range(6, STEP // 2):
        project_maps(p)
    for p in range(2, STEP // 2):
        add_up(p)


def away_kernel(core, xa_ref, xb_ref, t_ref, counts, images, maps, *refs):
    away_ref, rows_ref, mask_ref, next_maps, *next_tiles, sems = refs
    g = pl.program_id(0)
    half = len(next_tiles) * TILE
    mine = pl.ds(pl.multiple_of(core[0] * half, half), half)
    copies = [pltpu.make_async_copy(maps.at[mine], next_maps, sems.at[0])]
    for t, target in enumerate(next_tiles):
        place = pl.ds(pl.multiple_of(core[0] * half + t * TILE, TILE), TILE)
        copies.append(pltpu.make_async_copy(images.at[:, place, :], target, sems.at[1 + t]))

    @pl.when(g == 0)
    def _():
        for copy in copies:
            copy.start()
        for k in range(half):
            mine = valid_lanes(counts[core[0] * half + k], (1, mask_ref.shape[1]))
            mask_ref[k : k + 1] = jnp.where(mine, 1, 0)

    first = (1 - core[0]) * half + g * STEP
    valid = [valid_lanes(counts[first + k], t_ref.shape[1:]) for k in range(STEP)]
    sketch_step((xa_ref, xb_ref), t_ref, valid, rows_ref, away_ref, 0)

    @pl.when(g == pl.num_programs(0) - 1)
    def _():
        for copy in copies:
            copy.wait()


def kept_kernel(mask_ref, t_ref, *refs):
    tiles, (kept_ref, rows_ref) = refs[:-2], refs[-2:]
    half, rank, columns = kept_ref.shape
    for base in range(0, half, STEP):
        valid = [
            jnp.broadcast_to(mask_ref[k : k + 1], (rank, columns)) > 0
            for k in range(base, base + STEP)
        ]
        pair = tiles[base // TILE : base // TILE + 2]
        sketch_step(pair, t_ref, valid, rows_ref, kept_ref, base)


def sketch_away(core, counts, images, maps_t):
    count, blocks, columns = images.shape
    rank = maps_t.shape[1]
    half = blocks // 2
    steps = half // STEP
    tiles = half // TILE
    return pl.pallas_call(
        away_kernel,
        out_shape=[
            jax.ShapeDtypeStruct((half, rank, columns), BF16),
            jax.ShapeDtypeStruct((half, count, columns), BF16),
        ]
        + [jax.ShapeDtypeStruct((half, columns), jnp.int32)]
        + [jax.ShapeDtypeStruct((half, rank, columns), BF16)]
        + [jax.ShapeDtypeStruct((count, TILE, columns), BF16)] * tiles,
        grid_spec=pltpu.PrefetchScalarGridSpec(
            num_scalar_prefetch=1,
            grid=(steps,),
            in_specs=[
                pl.BlockSpec(
                    (count, TILE, columns), lambda g, s: (0, 2 * ((1 - s[0]) * steps + g), 0)
                ),
                pl.BlockSpec(
                    (count, TILE, columns), lambda g, s: (0, 2 * ((1 - s[0]) * steps + g) + 1, 0)
                ),
                pl.BlockSpec((STEP, rank, columns), lambda g, s: ((1 - s[0]) * steps + g, 0, 0)),
                pl.BlockSpec((blocks,), lambda g, s: (0,), memory_space=pltpu.SMEM),
                pl.BlockSpec(memory_space=pltpu.HBM),
                pl.BlockSpec(memory_space=pltpu.HBM),
            ],
            out_specs=[
                pl.BlockSpec((STEP, rank, columns), lambda g, s: (g, 0, 0)),
                pl.BlockSpec((STEP, count, columns), lambda g, s: (g, 0, 0)),
                pl.BlockSpec((half, columns), lambda g, s: (0, 0)),
            ]
            + [pl.BlockSpec(memory_space=pl.ANY)] * (tiles + 1),
            scratch_shapes=[pltpu.SemaphoreType.DMA((tiles + 1,))],
        ),
        compiler_params=pltpu.CompilerParams(vmem_limit_bytes=32 << 20),
        cost_estimate=pl.CostEstimate(flops=2**30, bytes_accessed=12 * 2**20, transcendentals=0),
        name="sketch_away",
    )(core, images, images, maps_t, counts, images, maps_t)


def sketch_kept(mask, maps, tiles):
    count, _, columns = tiles[0].shape
    half, rank, _ = maps.shape
    return pl.pallas_call(
        kept_kernel,
        out_shape=[
            jax.ShapeDtypeStruct((half, rank, columns), F32),
            jax.ShapeDtypeStruct((half, count, columns), BF16),
        ],
        compiler_params=pltpu.CompilerParams(vmem_limit_bytes=16 << 20),
        cost_estimate=pl.CostEstimate(flops=2**30, bytes_accessed=12 * 2**20, transcendentals=0),
        name="sketch_kept",
    )(mask, maps, *tiles)


def combine_kernel(parts_ref, out_ref):
    total = parts_ref[0].astype(F32)
    for i in range(1, parts_ref.shape[0]):
        total = total + parts_ref[i].astype(F32)
    rounded = total.astype(BF16)
    for c in range(out_ref.shape[0]):
        out_ref[c] = rounded


def combine(parts, copies):
    return pl.pallas_call(
        combine_kernel,
        out_shape=jax.ShapeDtypeStruct((copies,) + parts.shape[1:], BF16),
        compiler_params=pltpu.CompilerParams(vmem_limit_bytes=8 << 20),
        name="combine",
    )(parts)


def solve_kernel(parts_ref, out_ref):
    copies, own, rank, columns = out_ref.shape
    state = []
    for b in range(own):
        total = parts_ref[0, b].astype(F32)
        for i in range(1, parts_ref.shape[0]):
            total = total + parts_ref[i, b].astype(F32)
        gram = lax.dot_general(
            total, total, NT, precision=lax.Precision.HIGHEST, preferred_element_type=F32
        )
        state.append((total, gram, jnp.zeros((rank, columns), F32)))
    row = lax.broadcasted_iota(jnp.int32, (rank, columns), 0)
    for panel in range(0, rank, PANEL):
        for b in range(own):
            total, gram, scale = state[b]
            cols = [
                jnp.broadcast_to(gram[:, j : j + 1], (rank, columns))
                for j in range(panel, panel + PANEL)
            ]
            for t in range(PANEL):
                j = panel + t
                pivot = cols[t][j : j + 1, :]
                factor = jnp.where(row > j, cols[t] * (1.0 / pivot), 0.0)
                scale = jnp.where(row == j, lax.rsqrt(pivot), scale)
                total = total - factor * total[j : j + 1, :]
                for u in range(t + 1, PANEL):
                    cols[u] = cols[u] - factor * cols[u][j : j + 1, :]
                gram = gram - factor[:, :rank] * gram[j : j + 1, :]
            state[b] = (total, gram, scale)
    for b in range(own):
        rounded = (state[b][0] * state[b][2]).astype(BF16)
        for c in range(copies):
            out_ref[c, b] = rounded


def solve(parts, copies):
    return pl.pallas_call(
        solve_kernel,
        out_shape=jax.ShapeDtypeStruct((copies,) + parts.shape[1:], BF16),
        compiler_params=pltpu.CompilerParams(
            vmem_limit_bytes=8 << 20
        ),
        name="solve",
    )(parts)


def project_pair(rows_ref, bases_ref, k, out_ref):
    rank = bases_ref.shape[1]
    bases = diagonal(bases_ref[k], bases_ref[k + 1])
    pair = side_by_side(rows_ref, k)
    out = lax.dot_general(bases, pair, NT, preferred_element_type=F32).astype(BF16)
    out_ref[k] = out[:rank]
    out_ref[k + 1] = out[rank:]


def near_kernel(rows_ref, bases_ref, out_ref):
    blocks = bases_ref.shape[0]
    for k in range(0, blocks, 2):
        project_pair(rows_ref, bases_ref, k, out_ref)


def far_kernel(rows_ref, bases_ref, near_ref, out_hbm, out_buf, sems):
    blocks = bases_ref.shape[0]
    core = lax.axis_index("co")
    base = (1 - core) * blocks
    place = out_hbm.at[pl.ds(core * blocks, blocks)]
    copies = [pltpu.make_async_copy(near_ref, place, sems.at[0])]
    copies[0].start()
    for first in range(0, blocks, WRITE):
        for k in range(first, first + WRITE, 2):
            project_pair(rows_ref, bases_ref, k, out_buf)
        place = out_hbm.at[pl.ds(base + first, WRITE)]
        sem = sems.at[1 + first // WRITE]
        copies.append(pltpu.make_async_copy(out_buf.at[pl.ds(first, WRITE)], place, sem))
        copies[-1].start()
    for copy in copies:
        copy.wait()


def project(near_rows, far_rows, near, far):
    count = near_rows.shape[1]
    half, rank, columns = near.shape
    in_hbm, in_vmem = (pl.BlockSpec(memory_space=m) for m in (pltpu.HBM, pltpu.VMEM))
    settings = dict(
        compiler_params=pltpu.CompilerParams(vmem_limit_bytes=16 << 20),
        cost_estimate=pl.CostEstimate(flops=2**28, bytes_accessed=6 * 2**20, transcendentals=0),
    )
    done = pl.pallas_call(
        near_kernel,
        out_shape=jax.ShapeDtypeStruct((half, rank, count), BF16),
        in_specs=[in_vmem] * 2,
        out_specs=in_vmem,
        name="project_near",
        **settings,
    )(near_rows, near)
    return pl.pallas_call(
        far_kernel,
        out_shape=jax.ShapeDtypeStruct((2 * half, rank, count), BF16),
        in_specs=[in_vmem] * 3,
        out_specs=in_hbm,
        scratch_shapes=[
            pltpu.VMEM((half, rank, count), BF16),
            pltpu.SemaphoreType.DMA((1 + half // WRITE,)),
        ],
        name="project_far",
        **settings,
    )(far_rows, far, done)


def body(images, test_maps, counts):
    blocks, columns = images.shape[1], images.shape[2]
    rank = test_maps.shape[2]
    own = blocks // 32
    swap = [(0, 1), (1, 0)]
    maps_t = jnp.swapaxes(test_maps, 1, 2)
    images, maps_t, counts = [
        pltpu.with_memory_space_constraint(a, pltpu.HBM) for a in (images, maps_t, counts)
    ]
    core = lax.axis_index("co").astype(jnp.int32)[None]
    away, away_rows, mask, own_maps, *tiles = sketch_away(core, counts, images, maps_t)
    other = lax.ppermute(away, "co", swap)
    kept, kept_rows = sketch_kept(mask, own_maps, tiles)
    pair = (kept + other.astype(F32)).astype(BF16)
    parts = lax.all_to_all(pair, ("y", "x"), 0, 0, tiled=True)
    copies = combine(parts.reshape(16, own, rank, columns), 8)
    parts = lax.all_to_all(copies, ("zl", "zh"), 0, 0, tiled=True)
    copies = solve(parts, 16)
    near = lax.all_to_all(copies, ("y", "x"), 0, 0, tiled=True)
    near = near.reshape(blocks // 2, rank, columns)
    out = project(kept_rows, away_rows, near, lax.ppermute(near, "co", swap))
    return jnp.transpose(out, (2, 0, 1))


def solution(mesh):
    fine = Mesh(mesh.devices.reshape(4, 2, 2, 4, 4), AXES)
    in_specs = (P(AXES, None, None), P(), P())
    out_specs = P(AXES, None, None)
    return jax.shard_map(body, mesh=fine, in_specs=in_specs, out_specs=out_specs, check_vma=False)
```

```python
import functools

import jax
import jax.numpy as jnp
from jax import lax
from jax.experimental import pallas as pl
from jax.experimental.pallas import tpu as pltpu
from jax.sharding import Mesh, PartitionSpec as P

AXES = ("zl", "co", "zh", "x", "y")
F32, BF16 = jnp.float32, jnp.bfloat16
NT = (((1,), (1,)), ((), ()))
TILE = 8
STEP = 16
WRITE = 4
PANEL = 4
GROUP = 8


def valid_lanes(count, shape):
    position = lax.broadcasted_iota(jnp.int32, shape, len(shape) - 1) % (shape[-1] // 2)
    return position < count


def diagonal(upper, lower):
    zero = jnp.zeros_like(upper)
    return jnp.concatenate(
        [jnp.concatenate([upper, zero], 1), jnp.concatenate([zero, lower], 1)], 0
    )


def side_by_side(ref, k):
    return jnp.concatenate([ref[k], ref[k + 1]], 1)


def sketch_step(tiles, maps_ref, valid, rows_ref, sums_ref, base):
    rank, columns = maps_ref.shape[1:]
    sketches = [None] * (STEP // 2)

    def project_maps(p):
        maps = [
            jnp.where(valid[k], maps_ref[base + k], jnp.zeros((), BF16)) for k in (2 * p, 2 * p + 1)
        ]
        pair = side_by_side(rows_ref, base + 2 * p)
        sketch = lax.dot_general(diagonal(*maps), pair, NT, preferred_element_type=F32)
        sketches[p] = sketch.astype(BF16)

    def add_up(p):
        pair = side_by_side(rows_ref, base + 2 * p)
        both = jnp.dot(sketches[p], pair, preferred_element_type=F32)
        for h in range(2):
            own = both[h * rank : (h + 1) * rank, h * columns : (h + 1) * columns]
            own = jnp.where(valid[2 * p + h], own, 0.0)
            sums_ref[base + 2 * p + h] = own.astype(sums_ref.dtype)

    for h in (1, 0):
        rows_ref[base + h * TILE : base + (h + 1) * TILE] = pltpu.einshape("ikr->kir", tiles[h][...])
    for p in range(6):
        project_maps(p)
    for p in range(2):
        add_up(p)
    for p in range(6, STEP // 2):
        project_maps(p)
    for p in range(2, STEP // 2):
        add_up(p)


def away_kernel(core, xa_ref, xb_ref, t_ref, counts, images, maps, *refs):
    away_ref, rows_ref, mask_ref, next_maps, *next_tiles, sems = refs
    g = pl.program_id(0)
    half = len(next_tiles) * TILE
    mine = pl.ds(pl.multiple_of(core[0] * half, half), half)
    copies = [pltpu.make_async_copy(maps.at[mine], next_maps, sems.at[0])]
    for t, target in enumerate(next_tiles):
        place = pl.ds(pl.multiple_of(core[0] * half + t * TILE, TILE), TILE)
        copies.append(pltpu.make_async_copy(images.at[:, place, :], target, sems.at[1 + t]))

    @pl.when(g == 0)
    def _():
        for copy in copies:
            copy.start()
        for k in range(half):
            mine = valid_lanes(counts[core[0] * half + k], (1, mask_ref.shape[1]))
            mask_ref[k : k + 1] = jnp.where(mine, 1, 0)

    first = (1 - core[0]) * half + g * STEP
    valid = [valid_lanes(counts[first + k], t_ref.shape[1:]) for k in range(STEP)]
    sketch_step((xa_ref, xb_ref), t_ref, valid, rows_ref, away_ref, 0)

    @pl.when(g == pl.num_programs(0) - 1)
    def _():
        for copy in copies:
            copy.wait()


def kept_kernel(mask_ref, t_ref, *refs):
    tiles, (kept_ref, rows_ref) = refs[:-2], refs[-2:]
    half, rank, columns = kept_ref.shape
    for base in range(0, half, STEP):
        valid = [
            jnp.broadcast_to(mask_ref[k : k + 1], (rank, columns)) > 0
            for k in range(base, base + STEP)
        ]
        pair = tiles[base // TILE : base // TILE + 2]
        sketch_step(pair, t_ref, valid, rows_ref, kept_ref, base)


def sketch_away(core, counts, images, maps_t):
    count, blocks, columns = images.shape
    rank = maps_t.shape[1]
    half = blocks // 2
    steps = half // STEP
    tiles = half // TILE
    return pl.pallas_call(
        away_kernel,
        out_shape=[
            jax.ShapeDtypeStruct((half, rank, columns), BF16),
            jax.ShapeDtypeStruct((half, count, columns), BF16),
        ]
        + [jax.ShapeDtypeStruct((half, columns), jnp.int32)]
        + [jax.ShapeDtypeStruct((half, rank, columns), BF16)]
        + [jax.ShapeDtypeStruct((count, TILE, columns), BF16)] * tiles,
        grid_spec=pltpu.PrefetchScalarGridSpec(
            num_scalar_prefetch=1,
            grid=(steps,),
            in_specs=[
                pl.BlockSpec(
                    (count, TILE, columns), lambda g, s: (0, 2 * ((1 - s[0]) * steps + g), 0)
                ),
                pl.BlockSpec(
                    (count, TILE, columns), lambda g, s: (0, 2 * ((1 - s[0]) * steps + g) + 1, 0)
                ),
                pl.BlockSpec((STEP, rank, columns), lambda g, s: ((1 - s[0]) * steps + g, 0, 0)),
                pl.BlockSpec((blocks,), lambda g, s: (0,), memory_space=pltpu.SMEM),
                pl.BlockSpec(memory_space=pltpu.HBM),
                pl.BlockSpec(memory_space=pltpu.HBM),
            ],
            out_specs=[
                pl.BlockSpec((STEP, rank, columns), lambda g, s: (g, 0, 0)),
                pl.BlockSpec((STEP, count, columns), lambda g, s: (g, 0, 0)),
                pl.BlockSpec((half, columns), lambda g, s: (0, 0)),
            ]
            + [pl.BlockSpec(memory_space=pl.ANY)] * (tiles + 1),
            scratch_shapes=[pltpu.SemaphoreType.DMA((tiles + 1,))],
        ),
        compiler_params=pltpu.CompilerParams(vmem_limit_bytes=32 << 20),
        cost_estimate=pl.CostEstimate(flops=2**30, bytes_accessed=12 * 2**20, transcendentals=0),
        name="sketch_away",
    )(core, images, images, maps_t, counts, images, maps_t)


def sketch_kept(mask, maps, tiles):
    count, _, columns = tiles[0].shape
    half, rank, _ = maps.shape
    return pl.pallas_call(
        kept_kernel,
        out_shape=[
            jax.ShapeDtypeStruct((half, rank, columns), F32),
            jax.ShapeDtypeStruct((half, count, columns), BF16),
        ],
        compiler_params=pltpu.CompilerParams(vmem_limit_bytes=16 << 20),
        cost_estimate=pl.CostEstimate(flops=2**30, bytes_accessed=12 * 2**20, transcendentals=0),
        name="sketch_kept",
    )(mask, maps, *tiles)


def combine_kernel(parts_ref, out_ref):
    total = parts_ref[0].astype(F32)
    for i in range(1, parts_ref.shape[0]):
        total = total + parts_ref[i].astype(F32)
    rounded = total.astype(BF16)
    for c in range(out_ref.shape[0]):
        out_ref[c] = rounded


def combine(parts, copies):
    return pl.pallas_call(
        combine_kernel,
        out_shape=jax.ShapeDtypeStruct((copies,) + parts.shape[1:], BF16),
        compiler_params=pltpu.CompilerParams(vmem_limit_bytes=8 << 20),
        name="combine",
    )(parts)


def solve_kernel(parts_ref, out_ref):
    copies, own, rank, columns = out_ref.shape
    state = []
    for b in range(own):
        total = parts_ref[0, b].astype(F32)
        for i in range(1, parts_ref.shape[0]):
            total = total + parts_ref[i, b].astype(F32)
        gram = lax.dot_general(
            total, total, NT, precision=lax.Precision.HIGHEST, preferred_element_type=F32
        )
        state.append((total, gram, jnp.zeros((rank, columns), F32)))
    row = lax.broadcasted_iota(jnp.int32, (rank, columns), 0)
    finished = [[] for _ in range(own)]
    top = 0
    for panel in range(0, rank, PANEL):
        if panel - top == GROUP:
            for b in range(own):
                total, gram, scale = state[b]
                finished[b].append(total[:GROUP] * scale[:GROUP])
                state[b] = (total[GROUP:], gram[GROUP:], scale[GROUP:])
            row = row[GROUP:]
            top = panel
        for b in range(own):
            total, gram, scale = state[b]
            cols = [
                jnp.broadcast_to(gram[:, j : j + 1], (rank - top, columns))
                for j in range(panel, panel + PANEL)
            ]
            for t in range(PANEL):
                j = panel + t
                at = slice(j - top, j - top + 1)
                pivot = cols[t][at]
                factor = jnp.where(row > j, cols[t] * (1.0 / pivot), 0.0)
                scale = jnp.where(row == j, lax.rsqrt(pivot), scale)
                total = total - factor * total[at]
                for u in range(t + 1, PANEL):
                    cols[u] = cols[u] - factor * cols[u][at]
                gram = gram - factor[:, :rank] * gram[at]
            state[b] = (total, gram, scale)
    for b in range(own):
        total, _, scale = state[b]
        rounded = jnp.concatenate(finished[b] + [total * scale], 0).astype(BF16)
        for c in range(copies):
            out_ref[c, b] = rounded


def solve(parts, copies):
    return pl.pallas_call(
        solve_kernel,
        out_shape=jax.ShapeDtypeStruct((copies,) + parts.shape[1:], BF16),
        compiler_params=pltpu.CompilerParams(
            vmem_limit_bytes=8 << 20
        ),
        name="solve",
    )(parts)


def project_pair(rows_ref, bases_ref, k, out_ref):
    rank = bases_ref.shape[1]
    bases = diagonal(bases_ref[k], bases_ref[k + 1])
    pair = side_by_side(rows_ref, k)
    out = lax.dot_general(bases, pair, NT, preferred_element_type=F32).astype(BF16)
    out_ref[k] = out[:rank]
    out_ref[k + 1] = out[rank:]


def near_kernel(rows_ref, bases_ref, out_ref):
    blocks = bases_ref.shape[0]
    for k in range(0, blocks, 2):
        project_pair(rows_ref, bases_ref, k, out_ref)


def far_kernel(rows_ref, bases_ref, near_ref, out_hbm, out_buf, sems):
    blocks = bases_ref.shape[0]
    core = lax.axis_index("co")
    base = (1 - core) * blocks
    place = out_hbm.at[pl.ds(core * blocks, blocks)]
    copies = [pltpu.make_async_copy(near_ref, place, sems.at[0])]
    copies[0].start()
    for first in range(0, blocks, WRITE):
        for k in range(first, first + WRITE, 2):
            project_pair(rows_ref, bases_ref, k, out_buf)
        place = out_hbm.at[pl.ds(base + first, WRITE)]
        sem = sems.at[1 + first // WRITE]
        copies.append(pltpu.make_async_copy(out_buf.at[pl.ds(first, WRITE)], place, sem))
        copies[-1].start()
    for copy in copies:
        copy.wait()


def project(near_rows, far_rows, near, far):
    count = near_rows.shape[1]
    half, rank, columns = near.shape
    in_hbm, in_vmem = (pl.BlockSpec(memory_space=m) for m in (pltpu.HBM, pltpu.VMEM))
    settings = dict(
        compiler_params=pltpu.CompilerParams(vmem_limit_bytes=16 << 20),
        cost_estimate=pl.CostEstimate(flops=2**28, bytes_accessed=6 * 2**20, transcendentals=0),
    )
    done = pl.pallas_call(
        near_kernel,
        out_shape=jax.ShapeDtypeStruct((half, rank, count), BF16),
        in_specs=[in_vmem] * 2,
        out_specs=in_vmem,
        name="project_near",
        **settings,
    )(near_rows, near)
    return pl.pallas_call(
        far_kernel,
        out_shape=jax.ShapeDtypeStruct((2 * half, rank, count), BF16),
        in_specs=[in_vmem] * 3,
        out_specs=in_hbm,
        scratch_shapes=[
            pltpu.VMEM((half, rank, count), BF16),
            pltpu.SemaphoreType.DMA((1 + half // WRITE,)),
        ],
        name="project_far",
        **settings,
    )(far_rows, far, done)


def body(images, test_maps, counts):
    blocks, columns = images.shape[1], images.shape[2]
    rank = test_maps.shape[2]
    own = blocks // 32
    swap = [(0, 1), (1, 0)]
    maps_t = jnp.swapaxes(test_maps, 1, 2)
    images, maps_t, counts = [
        pltpu.with_memory_space_constraint(a, pltpu.HBM) for a in (images, maps_t, counts)
    ]
    core = lax.axis_index("co").astype(jnp.int32)[None]
    away, away_rows, mask, own_maps, *tiles = sketch_away(core, counts, images, maps_t)
    other = lax.ppermute(away, "co", swap)
    kept, kept_rows = sketch_kept(mask, own_maps, tiles)
    pair = (kept + other.astype(F32)).astype(BF16)
    parts = lax.all_to_all(pair, ("y", "x"), 0, 0, tiled=True)
    copies = combine(parts.reshape(16, own, rank, columns), 8)
    parts = lax.all_to_all(copies, ("zl", "zh"), 0, 0, tiled=True)
    copies = solve(parts, 16)
    near = lax.all_to_all(copies, ("y", "x"), 0, 0, tiled=True)
    near = near.reshape(blocks // 2, rank, columns)
    out = project(kept_rows, away_rows, near, lax.ppermute(near, "co", swap))
    return jnp.transpose(out, (2, 0, 1))


def solution(mesh):
    fine = Mesh(mesh.devices.reshape(4, 2, 2, 4, 4), AXES)
    in_specs = (P(AXES, None, None), P(), P())
    out_specs = P(AXES, None, None)
    return jax.shard_map(body, mesh=fine, in_specs=in_specs, out_specs=out_specs, check_vma=False)
```
